512 devices in a mesh: sub: 256 (over z, y, x), sep: 2 (over core).
Axes of the slice: x: 4, y: 8, z: 8, core: 2. Of those that a mesh axis runs over, the one named last changes fastest.
Arguments:
- sources: bfloat16 [256, 2, 768, 256], P('sub', 'sep'), may hold values from -6 to 6
- inner_inv: bfloat16 [256, 2, 768, 768], P('sub', 'sep'), as said below
- coupling: bfloat16 [256, 2, 512, 768], P('sub', 'sep'), may hold values from -0.0546875 to 0.0546875
- boundary_map: int32 [256, 2, 512], P('sub', 'sep'), may hold values from 0 to 479, as said below
- sep_inv_0: bfloat16 [256, 64, 64], P('sub', 'sep'), as said below
- sep_inv_1: bfloat16 [256, 128, 128], P('sub', 'sep'), as said below
- sep_inv_2: bfloat16 [256, 256, 256], P('sub', 'sep'), as said below
- sep_inv_3: bfloat16 [256, 512, 512], P('sub', 'sep'), as said below
- sep_couple_0: bfloat16 [256, 128, 64], P('sub', 'sep'), as said below
- sep_couple_1: bfloat16 [256, 256, 128], P('sub', 'sep'), as said below
- sep_couple_2: bfloat16 [256, 512, 256], P('sub', 'sep'), as said below
Outputs:
- inner_solution: bfloat16 [256, 2, 768, 256], P('sub', 'sep')
- sep_solution: bfloat16 [256, 2, 480, 256], P('sub', 'sep')
The draws below stay inside these ranges and needn't reach their ends.
Inputs may be any that keep to these rules, and one draw needn't show every extreme that they name: `boundary_map`: an entry m with (2^l - 1) * 32 <= m < (2^(l+1) - 1) * 32 names row m - (2^l - 1) * 32 of the leaf's own strip in the level-l separator above its subdomain. Every inner_inv[s, p] is lower triangular with a positive diagonal. Every sep_inv_0[s] is lower triangular with a positive diagonal, and equal for all s of one level-0 group. Every sep_inv_1[s] is lower triangular with a positive diagonal, and equal for all s of one level-1 group. Every sep_inv_2[s] is lower triangular with a positive diagonal, and equal for all s of one level-2 group. Every sep_inv_3[s] is lower triangular with a positive diagonal, and equal for all s of one level-3 group. sep_couple_0[s] is equal for all s of one level-0 group. sep_couple_1[s] is equal for all s of one level-1 group. sep_couple_2[s] is equal for all s of one level-2 group.
All inputs are finite; a program needn't handle non-finite values.
Results may differ from the reference program's by a relative error of at most 0.017.
Values may be sent and summed in bfloat16 or wider, within the bound.
A program may use at most 64 MiB of HBM per device.

```python
import math
import jax
import jax.numpy as jnp
from jax import lax

INNER = 768
BOUNDARY = 512
ROWS_0 = 32
SHOTS = 256
LEVELS = 4
SUBS = 256
STRIPS = 2
ORDER_0 = 64
ORDER_1 = 128
ORDER_2 = 256
ORDER_3 = 512
TOTAL_ROWS = 480


def lower_factor(key_lower, key_diagonal, leading, order):
    row_index = lax.broadcasted_iota(jnp.int32, (order, order), 0)
    col_index = lax.broadcasted_iota(jnp.int32, (order, order), 1)
    strict_lower = jnp.clip(jax.random.normal(key_lower, leading + (order, order), jnp.float32), -4.0, 4.0)
    diagonal = jax.random.uniform(key_diagonal, leading + (order, 1), jnp.float32, 0.5, 1.5)
    scaled = strict_lower * (0.8 / math.sqrt(order))
    return jnp.where(row_index > col_index, scaled, jnp.where(row_index == col_index, diagonal, 0.0))


def draw_inner_inv(key, part):
    base_key = jax.random.fold_in(key, 101)

    def draw_sub(index):
        sub_key = jax.random.fold_in(base_key, index)
        key_lower, key_diagonal = jax.random.split(sub_key)
        return lower_factor(key_lower, key_diagonal, (STRIPS,), INNER)
    return lax.map(draw_sub, jnp.arange(SUBS, dtype=jnp.int32)).astype(jnp.bfloat16)


def separator_level(key, height, order):
    members = min(4 ** (height + 1), SUBS)
    level_key = jax.random.fold_in(key, 200 + height)
    key_lower, key_diagonal = jax.random.split(level_key)
    blocks = lower_factor(key_lower, key_diagonal, (SUBS // members,), order)
    return jnp.repeat(blocks, members, axis=0)


def couple_level(key, height, parent_order, child_order):
    members = min(4 ** (height + 1), SUBS)
    level_key = jax.random.fold_in(key, 300 + height)
    block_shape = (SUBS // members, parent_order, child_order)
    dense = jnp.clip(jax.random.normal(level_key, block_shape, jnp.float32), -4.0, 4.0) * (0.35 / math.sqrt(child_order))
    return jnp.repeat(dense, members, axis=0)


def draw_sep_inv_0(key, part):
    return separator_level(key, 0, ORDER_0).astype(jnp.bfloat16)


def draw_sep_inv_1(key, part):
    return separator_level(key, 1, ORDER_1).astype(jnp.bfloat16)


def draw_sep_inv_2(key, part):
    return separator_level(key, 2, ORDER_2).astype(jnp.bfloat16)


def draw_sep_inv_3(key, part):
    return separator_level(key, 3, ORDER_3).astype(jnp.bfloat16)


def draw_sep_couple_0(key, part):
    return couple_level(key, 0, ORDER_1, ORDER_0).astype(jnp.bfloat16)


def draw_sep_couple_1(key, part):
    return couple_level(key, 1, ORDER_2, ORDER_1).astype(jnp.bfloat16)


def draw_sep_couple_2(key, part):
    return couple_level(key, 2, ORDER_3, ORDER_2).astype(jnp.bfloat16)


def draw_boundary_map(key, part):
    row_key = jax.random.fold_in(key, 401)
    return jax.random.randint(row_key, (SUBS, STRIPS, BOUNDARY), 0, TOTAL_ROWS, dtype=jnp.int32)


def steps_of(stream_key, extent, cuts, smallest, largest):
    level, own = 1.0, jax.random.fold_in(stream_key, 6)
    for dim, shards_of in cuts:
        draws = jnp.exp(jax.random.uniform(jax.random.fold_in(own, dim), (shards_of,), jnp.float32, smallest / len(cuts), largest / len(cuts)))
        level = level * jnp.repeat(draws, extent[dim] // shards_of).reshape([-1 if axis == dim else 1 for axis in range(len(extent))])
    return level


def gaussian(rng, shape, deviation, bound, cuts=(), held_as=jnp.bfloat16):
    values = deviation * jax.random.normal(rng, shape, jnp.float32)
    if cuts:
        values = values * steps_of(rng, shape, cuts, -0.22, 0.18)
    return jnp.clip(values, -bound, bound).astype(held_as)


def setup_inputs(seed: int = 0) -> dict:
    splits = jax.random.split(jax.random.key(seed), 12)
    return {
        "sources": gaussian(splits[0], (SUBS, STRIPS, INNER, SHOTS), 1.0, 6.0, ((0, 256), (1, 2))),
        "inner_inv": draw_inner_inv(jax.random.fold_in(splits[11], 71), 0),
        "coupling": gaussian(splits[2], (SUBS, STRIPS, BOUNDARY, INNER), (16 * INNER) ** -0.5, 0.0546875, ((0, 256), (1, 2))),
        "boundary_map": draw_boundary_map(jax.random.fold_in(splits[11], 71), 0),
        "sep_inv_0": draw_sep_inv_0(jax.random.fold_in(splits[11], 71), 0),
        "sep_inv_1": draw_sep_inv_1(jax.random.fold_in(splits[11], 71), 0),
        "sep_inv_2": draw_sep_inv_2(jax.random.fold_in(splits[11], 71), 0),
        "sep_inv_3": draw_sep_inv_3(jax.random.fold_in(splits[11], 71), 0),
        "sep_couple_0": draw_sep_couple_0(jax.random.fold_in(splits[11], 71), 0),
        "sep_couple_1": draw_sep_couple_1(jax.random.fold_in(splits[11], 71), 0),
        "sep_couple_2": draw_sep_couple_2(jax.random.fold_in(splits[11], 71), 0),
    }


def group_size(height):
    return min(4 ** (height + 1), SUBS)


def leaf_forward(pieces):
    source_rows, inverse, couple, targets = pieces
    inner_half = jnp.einsum('pik,pkn->pin', inverse.astype(jnp.float32), source_rows.astype(jnp.float32)).astype(jnp.bfloat16)
    boundary_half = jnp.einsum('pbk,pkn->pbn', couple.astype(jnp.float32), inner_half.astype(jnp.float32)).astype(jnp.bfloat16)
    slot_ids = jnp.arange(TOTAL_ROWS, dtype=jnp.int32)
    onehot = (targets[:, None, :] == slot_ids[None, :, None]).astype(jnp.float32)
    leaf_rows = jnp.einsum('prb,pbn->prn', onehot, boundary_half.astype(jnp.float32))
    return inner_half, leaf_rows


def leaf_backward(pieces):
    own_rows, targets, couple, inverse, inner_half = pieces
    picked = jax.vmap(lambda matrix, picks: jnp.take(matrix, picks, axis=0))(own_rows, targets)
    lifted = jnp.einsum('pbk,pbn->pkn', couple.astype(jnp.float32), picked.astype(jnp.float32)).astype(jnp.bfloat16)
    direct = jnp.einsum('pik,pin->pkn', inverse.astype(jnp.float32), inner_half.astype(jnp.float32))
    correction = jnp.einsum('pik,pin->pkn', inverse.astype(jnp.float32), lifted.astype(jnp.float32))
    return (direct - correction).astype(jnp.bfloat16)


def reference(sources, inner_inv, coupling, boundary_map, sep_inv_0, sep_inv_1, sep_inv_2, sep_inv_3, sep_couple_0, sep_couple_1, sep_couple_2):
    separators = [sep_inv_0, sep_inv_1, sep_inv_2, sep_inv_3]
    parents = [sep_couple_0, sep_couple_1, sep_couple_2]
    inner_half, leaf_rows = lax.map(leaf_forward, (sources, inner_inv, coupling, boundary_map))
    forward_rows = []
    child_term = None
    for height in range(LEVELS):
        size = ROWS_0 * 2 ** height
        start = ROWS_0 * (2 ** height - 1)
        members = group_size(height)
        groups = SUBS // members
        block = leaf_rows[:, :, start:start + size]
        rhs_rows = block.reshape(groups, members, STRIPS * size, SHOTS).sum(axis=1)
        if child_term is not None:
            rhs_rows = rhs_rows + child_term.reshape(groups, -1, STRIPS * size, SHOTS).sum(axis=1)
        rhs_half = rhs_rows.astype(jnp.bfloat16)
        matrix = separators[height][::members].astype(jnp.float32)
        solved = jnp.einsum('grk,gkn->grn', matrix, rhs_half.astype(jnp.float32)).astype(jnp.bfloat16)
        forward_rows.append(solved)
        if height < LEVELS - 1:
            child_term = jnp.einsum('grk,gkn->grn', parents[height][::members].astype(jnp.float32), solved.astype(jnp.float32))
    backward_rows = [None] * LEVELS
    for height in reversed(range(LEVELS)):
        members = group_size(height)
        matrix = separators[height][::members].astype(jnp.float32)
        if height == LEVELS - 1:
            target = forward_rows[height]
        else:
            fanout = group_size(height + 1) // members
            parent = jnp.repeat(backward_rows[height + 1], fanout, axis=0)
            back_term = jnp.einsum('grk,grn->gkn', parents[height][::members].astype(jnp.float32), parent.astype(jnp.float32))
            target = (forward_rows[height].astype(jnp.float32) - back_term).astype(jnp.bfloat16)
        backward_rows[height] = jnp.einsum('grk,grn->gkn', matrix, target.astype(jnp.float32)).astype(jnp.bfloat16)
    pieces = []
    for height in range(LEVELS):
        size = ROWS_0 * 2 ** height
        spread = jnp.repeat(backward_rows[height], group_size(height), axis=0)
        pieces.append(spread.reshape(SUBS, STRIPS, size, SHOTS))
    sep_solution = jnp.concatenate(pieces, axis=2)
    inner_solution = lax.map(leaf_backward, (sep_solution, boundary_map, coupling, inner_inv, inner_half))
    return (inner_solution, sep_solution)
```

```python
import functools

import jax
import jax.numpy as jnp
from jax import lax
from jax.experimental import pallas as pl
from jax.experimental.pallas import tpu as pltpu
from jax.sharding import PartitionSpec as P

MESH = pl.DeviceIdType.MESH
F32 = jnp.float32
BF16 = jnp.bfloat16
X, Y, Z, C = 4, 8, 8, 2
INNER, BOUND, SHOTS = 768, 512, 256
OWN = SHOTS // (X * C)
WIDE = 512


def mm(a, b):
    return lax.dot_general(a, b, (((1,), (0,)), ((), ())), preferred_element_type=F32)


def mm_nt(a, b):
    return lax.dot_general(a, b, (((1,), (1,)), ((), ())), preferred_element_type=F32)


def mm_tn(a, b):
    return lax.dot_general(a, b, (((0,), (0,)), ((), ())), preferred_element_type=F32)


def slots(shape, dim):
    at = lax.broadcasted_iota(jnp.int32, shape, dim)
    low = jnp.where(at < 448, at - 352, jnp.where(at < 480, at - 448, -1))
    return jnp.where(at < 256, at + 224, jnp.where(at < 384, at - 160, low))


def kernel(
    src_h, a_h, c_h, map_ref, s0_h, s1_h, s2_h, s3_h, k0_h, k1_h, k2_h,
    inner_ref, sep_ref,
    src, a, cm, s0, s1, s2, s3, k0, k1, k2,
    ih, lt, p1, w, xb, yb, e1, e2, g1, g2, g3, nn, direct,
    v3, v2, v1, b3, b2, b1, t3, t2, h3, h2, r3, r2, ob, dt,
    load_sem, fac_s, fac_r, p1_s, p1_r, p2_s, p2_r, p3_s, p3_r, p4_s, p4_r, p5_s, p5_r,
):
    sub = lax.axis_index("sub")
    core = lax.axis_index("sep")
    x = lax.rem(sub, X)
    y = lax.rem(sub // X, Y)
    z = sub // (X * Y)
    q = lax.rem(y, 4)
    quad = y - q
    own = x * C + core

    def at(xx, yy, zz, cc):
        return {"sub": zz * (X * Y) + yy * X + xx, "sep": cc}

    def x_peer(dx, dc):
        return lax.rem(x + dx, X), lax.rem(core + dc, C)

    def y_peer(j):
        return lax.rem(y + j, Y)

    def q_peer(j):
        return quad + lax.rem(q + j, 4)

    def z_peer(j):
        return lax.rem(z + j, Z)

    y_far = lax.rem(y + 4, Y)
    z_near = z + 1 - 2 * lax.rem(z, 2)
    lines = [(2, 0), (2, 1), (1, 0), (3, 0), (1, 1), (3, 1), (0, 1)]
    ring = [4, 3, 5, 2, 6, 1, 7]

    loads = [
        pltpu.make_async_copy(src_h, src, load_sem.at[0]),
        pltpu.make_async_copy(a_h, a, load_sem.at[1]),
        pltpu.make_async_copy(c_h, cm, load_sem.at[2]),
    ]
    facs = [(s0_h, s0), (s1_h, s1), (s2_h, s2), (s3_h, s3), (k0_h, k0), (k1_h, k1), (k2_h, k2)]
    for i, (h, v) in enumerate(facs):
        loads.append(pltpu.make_async_copy(h, v.at[core], load_sem.at[3 + i]))
    for copy in loads:
        copy.start()

    barrier = pltpu.get_barrier_semaphore()
    peers = [at(x_peer(dx, dc)[0], y, z, x_peer(dx, dc)[1]) for dx, dc in lines]
    peers += [at(x, y_peer(j), z, core) for j in ring]
    peers += [at(x, y, z_peer(j), core) for j in ring]
    peers += [at(x, y_far, z_near, core)]
    for peer in peers:
        pl.semaphore_signal(barrier, inc=1, device_id=peer, device_id_type=MESH)

    def send(source, target, s, r, peer):
        return pltpu.make_async_remote_copy(
            src_ref=source, dst_ref=target, send_sem=s, recv_sem=r, device_id=peer, device_id_type=MESH
        )

    onehot = (slots((WIDE, BOUND), 0) == map_ref[...]).astype(BF16)
    loads[0].wait()
    loads[1].wait()
    for i in range(3):
        lo, hi = 256 * i, 256 * (i + 1)
        ih[lo:hi, :] = mm(a[lo:hi, :hi], src[:hi, :]).astype(BF16)

    pl.semaphore_wait(barrier, len(peers))
    fac_copies = [
        send(h, v.at[core], fac_s.at[i], fac_r.at[i], at(x, y, z, 1 - core)) for i, (h, v) in enumerate(facs)
    ]
    for copy in fac_copies:
        copy.start()

    loads[2].wait()
    bh = mm(cm[...], ih[...])
    bht = bh.T.astype(BF16)
    lt[...] = mm_nt(bht, onehot).astype(BF16).reshape(X * C, OWN, WIDE)

    one = []
    for j, (dx, dc) in enumerate(lines):
        xx, cc = x_peer(dx, dc)
        one.append(send(lt.at[xx * C + cc], p1.at[own], p1_s.at[j], p1_r.at[j], at(xx, y, z, cc)))
    for copy in one:
        copy.start()
    p1[own] = lt[own]

    for copy in loads[3:]:
        copy.wait()
    for copy in fac_copies:
        copy.wait_recv()
    f0 = s0[...].reshape(64, 64)
    f1 = s1[...].reshape(128, 128)
    f2 = s2[...].reshape(256, 256)
    f3 = s3[...].reshape(512, 512)
    m0 = k0[...].reshape(128, 64)
    m1 = k1[...].reshape(256, 128)
    m2 = k2[...].reshape(512, 256)
    e0 = mm(m0, f0)
    e0t = e0.T.astype(BF16)
    e1[...] = mm(m1, f1).astype(BF16)
    e2[...] = mm(m2, f2).astype(BF16)
    g0 = mm_tn(f0, f0).astype(BF16)
    g1[...] = mm_tn(f1, f1).astype(BF16)
    g2[...] = mm_tn(f2, f2).astype(BF16)
    row = lax.broadcasted_iota(jnp.int32, (64, 128), 0)
    col = lax.broadcasted_iota(jnp.int32, (64, 128), 1)
    w[...] = jnp.zeros_like(w)
    yb[...] = jnp.zeros_like(yb)
    for p in range(2):
        w[128 * p : 128 * p + 64, :] = (col == row + 64 * p).astype(BF16)
        w[128 * p + 64 : 128 * p + 96, :] = e0t[32 * p : 32 * p + 32, :]
        part = jnp.concatenate([g0[32 * p : 32 * p + 32, 0:32], jnp.zeros((32, 32), BF16)], axis=1)
        other = jnp.concatenate([g0[32 * p : 32 * p + 32, 32:64], jnp.zeros((32, 32), BF16)], axis=1)
        blank = jnp.zeros((32, 64), BF16)
        yb[128 * p + 64 : 128 * p + 96, :] = jnp.concatenate([blank, part, blank, other], axis=1)
    wt = w[...].astype(F32).T
    lane = lax.rem(lax.broadcasted_iota(jnp.int32, (128, 256), 1), 128)
    xb[...] = jnp.where(lane < 64, wt, -wt).astype(BF16)

    for copy in one:
        copy.wait_recv()
    strips = []
    for p in range(2):
        total = p1[p].astype(F32)
        for xx in range(1, X):
            total = total + p1[xx * C + p].astype(F32)
        strips.append(total)
    tails = jnp.concatenate([strips[0][:, 384:], strips[1][:, 384:]], axis=1).astype(BF16)
    x1 = mm(tails, w[...])
    x1h = x1.astype(BF16)
    x2 = jnp.concatenate([strips[0][:, 256:384], strips[1][:, 256:384]], axis=1) + mm_nt(x1h, e1[...])
    x2h = x2.astype(BF16)
    x3 = jnp.concatenate([strips[0][:, :256], strips[1][:, :256]], axis=1) + mm_nt(x2h, e2[...])
    x3h = x3.astype(BF16)
    for k in range(8):
        v3[k] = x3h[16 * (k // 4) : 16 * (k // 4) + 16, 128 * (k % 4) : 128 * (k % 4) + 128]
    for k in range(4):
        v2[k] = x2h[16 * (k // 2) : 16 * (k // 2) + 16, 128 * (k % 2) : 128 * (k % 2) + 128]
    v1[...] = x1h

    two = []
    for j in ring:
        yy = y_peer(j)
        two.append(send(v3.at[yy], b3.at[j], p2_s.at[j], p2_r.at[j], at(x, yy, z, core)))
    for j in range(1, 4):
        yy = q_peer(j)
        two.append(send(v2.at[yy - quad], b2.at[j], p2_s.at[8 + j], p2_r.at[8 + j], at(x, yy, z, core)))
    for j in range(1, 4):
        two.append(send(v1, b1.at[j], p2_s.at[12 + j], p2_r.at[12 + j], at(x, q_peer(j), z, core)))
    for copy in two:
        copy.start()

    g3[...] = mm_tn(f3, f3).astype(BF16)

    for copy in two[:7]:
        copy.wait_recv()
    sum3 = v3[y].astype(F32)
    for j in range(1, 8):
        sum3 = sum3 + b3[j].astype(F32)
    t3[...] = sum3.astype(BF16)
    three = []
    for j in ring:
        three.append(send(t3, h3.at[j], p3_s.at[j], p3_r.at[j], at(x, y, z_peer(j), core)))
    for copy in three:
        copy.start()
    for copy in two[7:10]:
        copy.wait_recv()
    sum2 = v2[q].astype(F32)
    for j in range(1, 4):
        sum2 = sum2 + b2[j].astype(F32)
    t2[...] = sum2.astype(BF16)
    far = [(y_far, z), (y, z_near), (y_far, z_near)]
    for j, (yy, zz) in enumerate(far):
        three.append(send(t2, h2.at[j], p3_s.at[8 + j], p3_r.at[8 + j], at(x, yy, zz, core)))
        three[-1].start()

    for i in range(3):
        lo, hi = 256 * i, 256 * (i + 1)
        direct[lo:hi, :] = mm_tn(a[lo:, lo:hi], ih[lo:, :])
    picked_rows = mm(onehot, cm[...]).astype(BF16)
    for i in range(3):
        lo, hi = 256 * i, 256 * (i + 1)
        nn[lo:hi, :] = mm(picked_rows[:, lo:], a[lo:, lo:hi]).T.astype(BF16)
    out_slot = lax.broadcasted_iota(jnp.int32, (480, WIDE), 0)
    nn[INNER:, :] = (slots((480, WIDE), 1) == out_slot).astype(BF16)

    for copy in three[:7]:
        copy.wait_recv()
    top = t3[...].astype(F32)
    for j in range(1, 8):
        top = top + h3[j].astype(F32)
    r3[y] = top.astype(BF16)
    four = []
    for j in ring:
        four.append(send(r3.at[y], r3.at[y], p4_s.at[j], p4_r.at[j], at(x, y_peer(j), z, core)))
    for copy in four:
        copy.start()
    for copy in three[7:]:
        copy.wait_recv()
    mid = t2[...].astype(F32)
    for j in range(3):
        mid = mid + h2[j].astype(F32)
    r2[q] = mid.astype(BF16)
    for j in range(1, 4):
        four.append(send(r2.at[q], r2.at[q], p4_s.at[8 + j], p4_r.at[8 + j], at(x, q_peer(j), z, core)))
        four[-1].start()

    for copy in two[10:]:
        copy.wait_recv()
    low = v1[...].astype(F32)
    for j in range(1, 4):
        low = low + b1[j].astype(F32)
    own1 = mm(low.astype(BF16), g1[...])
    own0 = mm(tails, yb[...])
    for copy in four[7:]:
        copy.wait_recv()
    whole2 = jnp.concatenate(
        [jnp.concatenate([r2[2 * i], r2[2 * i + 1]], axis=1) for i in range(2)], axis=0
    )
    own2 = mm(whole2, g2[...])
    for copy in four[:7]:
        copy.wait_recv()
    whole3 = jnp.concatenate(
        [jnp.concatenate([r3[4 * i + k] for k in range(4)], axis=1) for i in range(2)], axis=0
    )
    d3 = mm(whole3, g3[...]).astype(BF16)
    d2 = (own2 - mm(d3, e2[...])).astype(BF16)
    d1 = (own1 - mm(d2, e1[...])).astype(BF16)
    d0 = (own0 + mm(d1, xb[...])).astype(BF16)
    for p in range(2):
        ob[p] = jnp.concatenate(
            [d3[:, 256 * p : 256 * p + 256], d2[:, 128 * p : 128 * p + 128], d0[:, 128 * p : 128 * p + 128]], axis=1
        )

    five = []
    for j, (dx, dc) in enumerate(lines):
        xx, cc = x_peer(dx, dc)
        five.append(send(ob.at[cc], dt.at[own], p5_s.at[j], p5_r.at[j], at(xx, y, z, cc)))
    for copy in five:
        copy.start()
    dt[own] = ob[core]
    for copy in five:
        copy.wait_recv()
    down = dt[...].reshape(SHOTS, WIDE)
    for i in range(3):
        lo, hi = 256 * i, 256 * (i + 1)
        inner_ref[lo:hi, :] = (direct[lo:hi, :] - mm_nt(nn[lo:hi, :], down)).astype(BF16)
    sep_ref[...] = mm_nt(nn[INNER:, :], down).astype(BF16)
    for copy in fac_copies + one + two + three + four + five:
        copy.wait_send()


def local(
    sources, inner_inv, coupling, boundary_map,
    sep_inv_0, sep_inv_1, sep_inv_2, sep_inv_3, sep_couple_0, sep_couple_1, sep_couple_2,
):
    hbm = pl.BlockSpec(memory_space=pl.ANY)
    vmem = pl.BlockSpec(memory_space=pltpu.VMEM)
    v = pltpu.VMEM
    dma = pltpu.SemaphoreType.DMA
    scratch = [
        v((INNER, SHOTS), BF16), v((INNER, INNER), BF16), v((BOUND, INNER), BF16),
        v((2, 32, 64), BF16), v((2, 64, 128), BF16), v((2, 128, 256), BF16), v((2, 256, 512), BF16),
        v((2, 64, 64), BF16), v((2, 128, 128), BF16), v((2, 256, 256), BF16),
        v((INNER, SHOTS), BF16), v((X * C, OWN, WIDE), BF16), v((X * C, OWN, WIDE), BF16),
        v((256, 128), BF16), v((128, 256), BF16), v((256, 256), BF16),
        v((256, 128), BF16), v((512, 256), BF16),
        v((128, 128), BF16), v((256, 256), BF16), v((512, 512), BF16),
        v((INNER + 480, WIDE), BF16), v((INNER, SHOTS), F32),
        v((8, 16, 128), BF16), v((4, 16, 128), BF16), v((32, 128), BF16),
        v((8, 16, 128), BF16), v((4, 16, 128), BF16), v((4, 32, 128), BF16),
        v((16, 128), BF16), v((16, 128), BF16), v((8, 16, 128), BF16), v((3, 16, 128), BF16),
        v((8, 16, 128), BF16), v((4, 16, 128), BF16),
        v((2, OWN, WIDE), BF16), v((X * C, OWN, WIDE), BF16),
        dma((10,)), dma((7,)), dma((7,)), dma((7,)), dma((7,)), dma((16,)), dma((16,)),
        dma((11,)), dma((11,)), dma((12,)), dma((12,)), dma((7,)), dma((7,)),
    ]
    inner, sep = pl.pallas_call(
        kernel,
        out_shape=(
            jax.ShapeDtypeStruct((INNER, SHOTS), BF16),
            jax.ShapeDtypeStruct((480, SHOTS), BF16),
        ),
        in_specs=[hbm, hbm, hbm, vmem] + [hbm] * 7,
        out_specs=(vmem, vmem),
        scratch_shapes=scratch,
        compiler_params=pltpu.CompilerParams(collective_id=0, has_side_effects=True),
    )(
        sources[0, 0], inner_inv[0, 0], coupling[0, 0], boundary_map[0],
        sep_inv_0[0], sep_inv_1[0], sep_inv_2[0], sep_inv_3[0],
        sep_couple_0[0], sep_couple_1[0], sep_couple_2[0],
    )
    return inner[None, None], sep[None, None]


def solution(mesh):
    leaf, factor = P("sub", "sep", None, None), P("sub", "sep", None)
    return jax.shard_map(
        local,
        mesh=mesh,
        in_specs=(leaf, leaf, leaf, factor) + (factor,) * 7,
        out_specs=(leaf, leaf),
        check_vma=False,
    )
```

```python
import functools

import jax
import jax.numpy as jnp
from jax import lax
from jax.experimental import pallas as pl
from jax.experimental.pallas import tpu as pltpu
from jax.sharding import PartitionSpec as P

MESH = pl.DeviceIdType.MESH
F32 = jnp.float32
BF16 = jnp.bfloat16
X, Y, Z, C = 4, 8, 8, 2
INNER, BOUND, SHOTS = 768, 512, 256
OWN = SHOTS // (X * C)
WIDE = 512


def mm(a, b):
    return lax.dot_general(a, b, (((1,), (0,)), ((), ())), preferred_element_type=F32)


def mm_nt(a, b):
    return lax.dot_general(a, b, (((1,), (1,)), ((), ())), preferred_element_type=F32)


def mm_tn(a, b):
    return lax.dot_general(a, b, (((0,), (0,)), ((), ())), preferred_element_type=F32)


def slots(shape, dim):
    at = lax.broadcasted_iota(jnp.int32, shape, dim)
    low = jnp.where(at < 448, at - 352, jnp.where(at < 480, at - 448, -1))
    return jnp.where(at < 256, at + 224, jnp.where(at < 384, at - 160, low))


def kernel(
    src_h, a_h, c_h, map_h, s0_h, s1_h, s2_h, s3_h, k0_h, k1_h, k2_h,
    inner_ref, sep_ref,
    src, a, cm, mp, s0, s1, s2, s3, k0, k1, k2,
    ih, lt3, ltr, p3, pr, w, xb, yb, e1, e2, g1, g2, g3, nn, direct,
    v3, v2, v1, b3, b2, b1, t3, t2, h3, h2, r3, r2, o3, orr, d3a, dra,
    load_sem, fac_s, fac_r, p1_s, p1_r, p2_s, p2_r, p3_s, p3_r, p4_s, p4_r, p5_s, p5_r,
):
    sub = lax.axis_index("sub")
    core = lax.axis_index("sep")
    x = lax.rem(sub, X)
    y = lax.rem(sub // X, Y)
    z = sub // (X * Y)
    q = lax.rem(y, 4)
    quad = y - q
    own = x * C + core

    def at(xx, yy, zz, cc):
        return {"sub": zz * (X * Y) + yy * X + xx, "sep": cc}

    def x_peer(dx, dc):
        return lax.rem(x + dx, X), lax.rem(core + dc, C)

    def y_peer(j):
        return lax.rem(y + j, Y)

    def q_peer(j):
        return quad + lax.rem(q + j, 4)

    def z_peer(j):
        return lax.rem(z + j, Z)

    z_near = z + 1 - 2 * lax.rem(z, 2)
    lines = [(2, 0), (2, 1), (1, 0), (3, 0), (1, 1), (3, 1), (0, 1)]
    ring = [4, 3, 5, 2, 6, 1, 7]

    barrier = pltpu.get_barrier_semaphore()
    peers = [at(x, y, z_peer(j), core) for j in ring]
    peers += [at(x, y_peer(j), z, core) for j in ring]
    peers += [at(x_peer(dx, dc)[0], y, z, x_peer(dx, dc)[1]) for dx, dc in lines]
    for peer in peers:
        pl.semaphore_signal(barrier, inc=1, device_id=peer, device_id_type=MESH)

    loads = [pltpu.make_async_copy(map_h, mp, load_sem.at[0])]
    loads.append(pltpu.make_async_copy(src_h, src, load_sem.at[1]))
    for i in range(3):
        lo, hi = 256 * i, 256 * (i + 1)
        loads.append(pltpu.make_async_copy(a_h.at[lo:hi, :hi], a.at[lo:hi, :hi], load_sem.at[2 + i]))
    loads.append(pltpu.make_async_copy(c_h, cm, load_sem.at[5]))
    facs = [(s0_h, s0), (s1_h, s1), (s2_h, s2), (s3_h, s3), (k0_h, k0), (k1_h, k1), (k2_h, k2)]
    for i, (h, v) in enumerate(facs):
        loads.append(pltpu.make_async_copy(h, v.at[core], load_sem.at[6 + i]))
    for copy in loads:
        copy.start()

    def send(source, target, s, r, peer):
        return pltpu.make_async_remote_copy(
            src_ref=source, dst_ref=target, send_sem=s, recv_sem=r, device_id=peer, device_id_type=MESH
        )

    loads[0].wait()
    onehot = (slots((WIDE, BOUND), 0) == mp[...]).astype(BF16)
    loads[1].wait()
    for i in range(3):
        lo, hi = 256 * i, 256 * (i + 1)
        loads[2 + i].wait()
        ih[lo:hi, :] = mm(a[lo:hi, :hi], src[:hi, :]).astype(BF16)
    loads[5].wait()
    bh = mm(cm[...], ih[...])
    bht = bh.T.astype(BF16)
    ltr[...] = mm_nt(bht, onehot[256:, :]).astype(BF16).reshape(X * C, OWN, 256)
    pl.semaphore_wait(barrier, len(peers))

    one = []
    for half, (source, target) in enumerate([(ltr, pr), (lt3, p3)]):
        for j, (dx, dc) in enumerate(lines):
            xx, cc = x_peer(dx, dc)
            k = 7 * half + j
            one.append(send(source.at[xx * C + cc], target.at[own], p1_s.at[k], p1_r.at[k], at(xx, y, z, cc)))
    for copy in one[:7]:
        copy.start()
    lt3[...] = mm_nt(bht, onehot[:256, :]).astype(BF16).reshape(X * C, OWN, 256)
    for copy in one[7:]:
        copy.start()
    fac_copies = [
        send(h, v.at[core], fac_s.at[i], fac_r.at[i], at(x, y, z, 1 - core)) for i, (h, v) in enumerate(facs)
    ]
    for copy in fac_copies:
        copy.start()
    pr[own] = ltr[own]
    p3[own] = lt3[own]

    for copy in loads[6:]:
        copy.wait()
    for copy in fac_copies:
        copy.wait_recv()
    f0 = s0[...].reshape(64, 64)
    f1 = s1[...].reshape(128, 128)
    f2 = s2[...].reshape(256, 256)
    f3 = s3[...].reshape(512, 512)
    m0 = k0[...].reshape(128, 64)
    m1 = k1[...].reshape(256, 128)
    m2 = k2[...].reshape(512, 256)
    e0 = mm(m0, f0)
    e0t = e0.T.astype(BF16)
    e1[...] = mm(m1, f1).astype(BF16)
    e2[...] = mm(m2, f2).astype(BF16)
    w[...] = jnp.zeros_like(w)
    row = lax.broadcasted_iota(jnp.int32, (64, 128), 0)
    col = lax.broadcasted_iota(jnp.int32, (64, 128), 1)
    for p in range(2):
        w[128 * p : 128 * p + 64, :] = (col == row + 64 * p).astype(BF16)
        w[128 * p + 64 : 128 * p + 96, :] = e0t[32 * p : 32 * p + 32, :]

    def line_sum(buffer, p):
        total = buffer[p].astype(F32)
        for xx in range(1, X):
            total = total + buffer[xx * C + p].astype(F32)
        return total

    for copy in one[:7]:
        copy.wait_recv()
    rest = [line_sum(pr, p) for p in range(2)]
    tails = jnp.concatenate([rest[0][:, 128:], rest[1][:, 128:]], axis=1).astype(BF16)
    x1h = mm(tails, w[...]).astype(BF16)
    x2 = jnp.concatenate([rest[0][:, :128], rest[1][:, :128]], axis=1) + mm_nt(x1h, e1[...])
    x2h = x2.astype(BF16)
    x3 = mm_nt(x2h, e2[...])
    for k in range(4):
        v2[k] = x2h[16 * (k // 2) : 16 * (k // 2) + 16, 128 * (k % 2) : 128 * (k % 2) + 128]
    v1[...] = x1h
    for copy in one[7:]:
        copy.wait_recv()
    x3h = (x3 + jnp.concatenate([line_sum(p3, 0), line_sum(p3, 1)], axis=1)).astype(BF16)
    for k in range(8):
        v3[k] = x3h[16 * (k // 4) : 16 * (k // 4) + 16, 128 * (k % 4) : 128 * (k % 4) + 128]

    two = []
    for j in ring:
        yy = y_peer(j)
        two.append(send(v3.at[yy], b3.at[j], p2_s.at[j], p2_r.at[j], at(x, yy, z, core)))
    for j in ring:
        yy = y_peer(j)
        two.append(send(v2.at[lax.rem(yy, 4)], b2.at[j], p2_s.at[8 + j], p2_r.at[8 + j], at(x, yy, z, core)))
    for j in range(1, 4):
        two.append(send(v1, b1.at[j], p2_s.at[16 + j], p2_r.at[16 + j], at(x, q_peer(j), z, core)))
    for copy in two[:14]:
        copy.start()

    g0 = mm_tn(f0, f0).astype(BF16)
    g1[...] = mm_tn(f1, f1).astype(BF16)
    g2[...] = mm_tn(f2, f2).astype(BF16)
    g3[...] = mm_tn(f3, f3).astype(BF16)
    yb[...] = jnp.zeros_like(yb)
    blank = jnp.zeros((32, 64), BF16)
    gap = jnp.zeros((32, 32), BF16)
    for p in range(2):
        rows = g0[32 * p : 32 * p + 32, :]
        yb[128 * p + 64 : 128 * p + 96, :] = jnp.concatenate([blank, rows[:, :32], gap, blank, rows[:, 32:], gap], axis=1)
    wt = w[...].astype(F32).T
    lane = lax.rem(lax.broadcasted_iota(jnp.int32, (128, 256), 1), 128)
    xb[...] = jnp.where(lane < 64, wt, -wt).astype(BF16)

    for copy in two[:7]:
        copy.wait_recv()
    sum3 = v3[y].astype(F32)
    for j in range(1, 8):
        sum3 = sum3 + b3[j].astype(F32)
    t3[...] = sum3.astype(BF16)
    three = []
    for j in ring:
        three.append(send(t3, h3.at[j], p3_s.at[j], p3_r.at[j], at(x, y, z_peer(j), core)))
    for copy in three:
        copy.start()
    for copy in two[7:14]:
        copy.wait_recv()
    sum2 = v2[q].astype(F32)
    for j in range(1, 8):
        sum2 = sum2 + b2[j].astype(F32)
    t2[...] = sum2.astype(BF16)
    three.append(send(t2, h2, p3_s.at[8], p3_r.at[8], at(x, y, z_near, core)))
    three[-1].start()
    for copy in two[14:]:
        copy.start()

    for i in range(3):
        lo, hi = 256 * i, 256 * (i + 1)
        direct[lo:hi, :] = mm_tn(a[lo:, lo:hi], ih[lo:, :])
    picked_rows = mm(onehot, cm[...]).astype(BF16)
    for i in range(3):
        lo, hi = 256 * i, 256 * (i + 1)
        nn[lo:hi, :] = mm(picked_rows[:, lo:], a[lo:, lo:hi]).T.astype(BF16)
    out_slot = lax.broadcasted_iota(jnp.int32, (480, WIDE), 0)
    nn[INNER:, :] = (slots((480, WIDE), 1) == out_slot).astype(BF16)

    for copy in three[:7]:
        copy.wait_recv()
    top = t3[...].astype(F32)
    for j in range(1, 8):
        top = top + h3[j].astype(F32)
    r3[y] = top.astype(BF16)
    four = []
    for j in ring:
        four.append(send(r3.at[y], r3.at[y], p4_s.at[j], p4_r.at[j], at(x, y_peer(j), z, core)))
    for copy in four:
        copy.start()
    three[7].wait_recv()
    r2[q] = (t2[...].astype(F32) + h2[...].astype(F32)).astype(BF16)
    for j in range(1, 4):
        four.append(send(r2.at[q], r2.at[q], p4_s.at[8 + j], p4_r.at[8 + j], at(x, q_peer(j), z, core)))
        four[-1].start()

    for copy in two[14:]:
        copy.wait_recv()
    low = v1[...].astype(F32)
    for j in range(1, 4):
        low = low + b1[j].astype(F32)
    own1 = mm(low.astype(BF16), g1[...])
    own0 = mm(tails, yb[...])
    for copy in four[7:]:
        copy.wait_recv()
    whole2 = jnp.concatenate(
        [jnp.concatenate([r2[2 * i], r2[2 * i + 1]], axis=1) for i in range(2)], axis=0
    )
    own2 = mm(whole2, g2[...])
    for copy in four[:7]:
        copy.wait_recv()
    whole3 = jnp.concatenate(
        [jnp.concatenate([r3[4 * i + k] for k in range(4)], axis=1) for i in range(2)], axis=0
    )
    d3 = mm(whole3, g3[...]).astype(BF16)
    for p in range(2):
        o3[p] = d3[:, 256 * p : 256 * p + 256]

    five = []
    for half, (source, target) in enumerate([(o3, d3a), (orr, dra)]):
        for j, (dx, dc) in enumerate(lines):
            xx, cc = x_peer(dx, dc)
            k = 7 * half + j
            five.append(send(source.at[cc], target.at[own], p5_s.at[k], p5_r.at[k], at(xx, y, z, cc)))
    for copy in five[:7]:
        copy.start()
    d3a[own] = o3[core]
    d2 = (own2 - mm(d3, e2[...])).astype(BF16)
    d1 = (own1 - mm(d2, e1[...])).astype(BF16)
    d0 = (own0 + mm(d1, xb[...])).astype(BF16)
    for p in range(2):
        orr[p] = jnp.concatenate([d2[:, 128 * p : 128 * p + 128], d0[:, 128 * p : 128 * p + 128]], axis=1)
    for copy in five[7:]:
        copy.start()
    dra[own] = orr[core]
    for copy in five[:7]:
        copy.wait_recv()
    down3 = d3a[...].reshape(SHOTS, 256)
    for i in range(3):
        lo, hi = 256 * i, 256 * (i + 1)
        direct[lo:hi, :] = direct[lo:hi, :] - mm_nt(nn[lo:hi, :256], down3)
    sep_ref[224:, :] = mm_nt(nn[INNER + 224 :, :256], down3).astype(BF16)
    for copy in five[7:]:
        copy.wait_recv()
    downr = dra[...].reshape(SHOTS, 256)
    for i in range(3):
        lo, hi = 256 * i, 256 * (i + 1)
        inner_ref[lo:hi, :] = (direct[lo:hi, :] - mm_nt(nn[lo:hi, 256:], downr)).astype(BF16)
    sep_ref[:224, :] = mm_nt(nn[INNER : INNER + 224, 256:], downr).astype(BF16)
    for copy in fac_copies + one + two + three + four + five:
        copy.wait_send()


def write_out(inner, sep, inner_h, sep_h, sem):
    copies = [
        pltpu.make_async_copy(inner, inner_h, sem.at[0]),
        pltpu.make_async_copy(sep, sep_h, sem.at[1]),
    ]
    for copy in copies:
        copy.start()
    for copy in copies:
        copy.wait()


def local(
    sources, inner_inv, coupling, boundary_map,
    sep_inv_0, sep_inv_1, sep_inv_2, sep_inv_3, sep_couple_0, sep_couple_1, sep_couple_2,
):
    held = [
        sources[0, 0], inner_inv[0, 0], coupling[0, 0], boundary_map[0],
        sep_inv_0[0], sep_inv_1[0], sep_inv_2[0], sep_inv_3[0],
        sep_couple_0[0], sep_couple_1[0], sep_couple_2[0],
    ]
    held = [pltpu.with_memory_space_constraint(v, pltpu.HBM) for v in held]
    hbm = pl.BlockSpec(memory_space=pltpu.HBM)
    vmem = pl.BlockSpec(memory_space=pltpu.VMEM)
    v = pltpu.VMEM
    dma = pltpu.SemaphoreType.DMA
    piece = v((X * C, OWN, 256), BF16)
    scratch = [
        v((INNER, SHOTS), BF16), v((INNER, INNER), BF16), v((BOUND, INNER), BF16), v((1, BOUND), jnp.int32),
        v((2, 32, 64), BF16), v((2, 64, 128), BF16), v((2, 128, 256), BF16), v((2, 256, 512), BF16),
        v((2, 64, 64), BF16), v((2, 128, 128), BF16), v((2, 256, 256), BF16),
        v((INNER, SHOTS), BF16), piece, piece, piece, piece,
        v((256, 128), BF16), v((128, 256), BF16), v((256, 256), BF16),
        v((256, 128), BF16), v((512, 256), BF16),
        v((128, 128), BF16), v((256, 256), BF16), v((512, 512), BF16),
        v((INNER + 480, WIDE), BF16), v((INNER, SHOTS), F32),
        v((8, 16, 128), BF16), v((4, 16, 128), BF16), v((32, 128), BF16),
        v((8, 16, 128), BF16), v((8, 16, 128), BF16), v((4, 32, 128), BF16),
        v((16, 128), BF16), v((16, 128), BF16), v((8, 16, 128), BF16), v((16, 128), BF16),
        v((8, 16, 128), BF16), v((4, 16, 128), BF16),
        v((2, OWN, 256), BF16), v((2, OWN, 256), BF16), piece, piece,
        dma((13,)), dma((7,)), dma((7,)), dma((14,)), dma((14,)), dma((20,)), dma((20,)),
        dma((9,)), dma((9,)), dma((12,)), dma((12,)), dma((14,)), dma((14,)),
    ]
    inner, sep = pl.pallas_call(
        kernel,
        out_shape=(
            jax.ShapeDtypeStruct((INNER, SHOTS), BF16),
            jax.ShapeDtypeStruct((480, SHOTS), BF16),
        ),
        in_specs=[hbm] * 11,
        out_specs=(vmem, vmem),
        scratch_shapes=scratch,
        compiler_params=pltpu.CompilerParams(
            collective_id=0, has_side_effects=True, vmem_limit_bytes=24 * 1024 * 1024
        ),
    )(*held)
    inner, sep = pl.pallas_call(
        write_out,
        out_shape=(
            jax.ShapeDtypeStruct((INNER, SHOTS), BF16),
            jax.ShapeDtypeStruct((480, SHOTS), BF16),
        ),
        in_specs=[vmem] * 2,
        out_specs=(pl.BlockSpec(memory_space=pltpu.HBM),) * 2,
        scratch_shapes=[dma((2,))],
        compiler_params=pltpu.CompilerParams(vmem_limit_bytes=8 * 1024 * 1024),
    )(inner, sep)
    return inner[None, None], sep[None, None]


def solution(mesh):
    leaf, factor = P("sub", "sep", None, None), P("sub", "sep", None)
    return jax.shard_map(
        local,
        mesh=mesh,
        in_specs=(leaf, leaf, leaf, factor) + (factor,) * 7,
        out_specs=(leaf, leaf),
        check_vma=False,
    )
```

```python
import functools

import jax
import jax.numpy as jnp
from jax import lax
from jax.experimental import pallas as pl
from jax.experimental.pallas import tpu as pltpu
from jax.sharding import PartitionSpec as P

MESH = pl.DeviceIdType.MESH
F32 = jnp.float32
BF16 = jnp.bfloat16
X, Y, Z, C = 4, 8, 8, 2
INNER, BOUND, SHOTS = 768, 512, 256
OWN = SHOTS // (X * C)
WIDE = 512


def mm(a, b):
    return lax.dot_general(a, b, (((1,), (0,)), ((), ())), preferred_element_type=F32)


def mm_nt(a, b):
    return lax.dot_general(a, b, (((1,), (1,)), ((), ())), preferred_element_type=F32)


def mm_tn(a, b):
    return lax.dot_general(a, b, (((0,), (0,)), ((), ())), preferred_element_type=F32)


def slots(shape, dim):
    at = lax.broadcasted_iota(jnp.int32, shape, dim)
    low = jnp.where(at < 448, at - 352, jnp.where(at < 480, at - 448, -1))
    return jnp.where(at < 256, at + 224, jnp.where(at < 384, at - 160, low))


def kernel(
    src_h, a_h, c_h, map_h, s0_h, s1_h, s2_h, s3_h, k0_h, k1_h, k2_h,
    inner_ref, sep_ref,
    src, a, cm, mp, s0, s1, s2, s3, k0, k1, k2,
    ih, lt3, ltr, p3, pr, w, xb, yb, e1, e2, g1, g2, g3, nn, direct,
    tl, q3, v3, v2, v1, b3, b2, b1, t3, t2, h3, h2, r3, r2, o3, orr, d3a, dra,
    far_sem, load_sem, fac_s, fac_r, p1_s, p1_r, p2_s, p2_r, p3_s, p3_r, p4_s, p4_r, p5_s, p5_r,
):
    sub = lax.axis_index("sub")
    core = lax.axis_index("sep")
    x = lax.rem(sub, X)
    y = lax.rem(sub // X, Y)
    z = sub // (X * Y)
    q = lax.rem(y, 4)
    quad = y - q
    own = x * C + core

    def at(xx, yy, zz, cc):
        return {"sub": zz * (X * Y) + yy * X + xx, "sep": cc}

    def x_peer(dx, dc):
        return lax.rem(x + dx, X), lax.rem(core + dc, C)

    def y_peer(j):
        return lax.rem(y + j, Y)

    def q_peer(j):
        return quad + lax.rem(q + j, 4)

    def z_peer(j):
        return lax.rem(z + j, Z)

    z_near = z + 1 - 2 * lax.rem(z, 2)
    lines = [(2, 0), (2, 1), (1, 0), (3, 0), (1, 1), (3, 1), (0, 1)]
    ring = [4, 3, 5, 2, 6, 1, 7]

    barrier = pltpu.get_barrier_semaphore()
    near = [2, 6, 1, 7]
    peers = [at(x_peer(dx, dc)[0], y, z, x_peer(dx, dc)[1]) for dx, dc in lines[:2]]
    peers += [at(x, y, z_peer(j), core) for j in near]
    peers += [at(x, y_peer(j), z, core) for j in near]
    peers += [at(x_peer(dx, dc)[0], y, z, x_peer(dx, dc)[1]) for dx, dc in lines[2:]]
    for peer in peers:
        pl.semaphore_signal(barrier, inc=1, device_id=peer, device_id_type=MESH)

    loads = [pltpu.make_async_copy(map_h, mp, load_sem.at[0])]
    loads.append(pltpu.make_async_copy(src_h, src, load_sem.at[1]))
    for i in range(3):
        lo, hi = 256 * i, 256 * (i + 1)
        loads.append(pltpu.make_async_copy(a_h.at[lo:hi, :hi], a.at[lo:hi, :hi], load_sem.at[2 + i]))
    loads.append(pltpu.make_async_copy(c_h, cm, load_sem.at[5]))
    facs = [(s0_h, s0), (s1_h, s1), (s2_h, s2), (s3_h, s3), (k0_h, k0), (k1_h, k1), (k2_h, k2)]
    for i, (h, v) in enumerate(facs):
        loads.append(pltpu.make_async_copy(h, v.at[core], load_sem.at[6 + i]))
    for copy in loads:
        copy.start()

    def send(source, target, s, r, peer):
        return pltpu.make_async_remote_copy(
            src_ref=source, dst_ref=target, send_sem=s, recv_sem=r, device_id=peer, device_id_type=MESH
        )

    loads[0].wait()
    onehot = (slots((WIDE, BOUND), 0) == mp[...]).astype(BF16)
    loads[1].wait()
    for i in range(3):
        lo, hi = 256 * i, 256 * (i + 1)
        loads[2 + i].wait()
        ih[lo:hi, :] = mm(a[lo:hi, :hi], src[:hi, :]).astype(BF16)
    loads[5].wait()
    bh = mm(cm[...], ih[...])
    bht = bh.T.astype(BF16)
    ltr[...] = mm_nt(bht, onehot[256:, :]).astype(BF16).reshape(X * C, OWN, 256)
    pl.semaphore_wait(barrier, len(peers))

    one = []
    for half, (source, target) in enumerate([(ltr, pr), (lt3, p3)]):
        for j, (dx, dc) in enumerate(lines):
            xx, cc = x_peer(dx, dc)
            k = 7 * half + j
            one.append(send(source.at[xx * C + cc], target.at[own], p1_s.at[k], p1_r.at[k], at(xx, y, z, cc)))
    for copy in one[:7]:
        copy.start()
    lt3[...] = mm_nt(bht, onehot[:256, :]).astype(BF16).reshape(X * C, OWN, 256)
    for copy in one[7:]:
        copy.start()
    for peer in [at(x, y, z_peer(2), core), at(x, y, z_peer(6), core), at(x, y_peer(2), z, core), at(x, y_peer(6), z, core)]:
        pl.semaphore_signal(far_sem, inc=1, device_id=peer, device_id_type=MESH)
    fac_copies = [
        send(h, v.at[core], fac_s.at[i], fac_r.at[i], at(x, y, z, 1 - core)) for i, (h, v) in enumerate(facs)
    ]
    for copy in fac_copies:
        copy.start()
    pr[own] = ltr[own]
    p3[own] = lt3[own]

    for copy in loads[6:]:
        copy.wait()
    for copy in fac_copies:
        copy.wait_recv()
    f0 = s0[...].reshape(64, 64)
    f1 = s1[...].reshape(128, 128)
    f2 = s2[...].reshape(256, 256)
    f3 = s3[...].reshape(512, 512)
    m0 = k0[...].reshape(128, 64)
    m1 = k1[...].reshape(256, 128)
    m2 = k2[...].reshape(512, 256)
    e0 = mm(m0, f0)
    e0t = e0.T.astype(BF16)
    e1[...] = mm(m1, f1).astype(BF16)
    e2[...] = mm(m2, f2).astype(BF16)
    w[...] = jnp.zeros_like(w)
    row = lax.broadcasted_iota(jnp.int32, (64, 128), 0)
    col = lax.broadcasted_iota(jnp.int32, (64, 128), 1)
    for p in range(2):
        w[128 * p : 128 * p + 64, :] = (col == row + 64 * p).astype(BF16)
        w[128 * p + 64 : 128 * p + 96, :] = e0t[32 * p : 32 * p + 32, :]

    def line_sum(buffer, p):
        total = buffer[p].astype(F32)
        for xx in range(1, X):
            total = total + buffer[xx * C + p].astype(F32)
        return total

    for copy in one[:7]:
        copy.wait_recv()

    @pl.when(sub >= 0)
    def _():
        rest = [line_sum(pr, p) for p in range(2)]
        tails = jnp.concatenate([rest[0][:, 128:], rest[1][:, 128:]], axis=1).astype(BF16)
        tl[...] = tails
        x1h = mm(tails, w[...]).astype(BF16)
        x2 = jnp.concatenate([rest[0][:, :128], rest[1][:, :128]], axis=1) + mm_nt(x1h, e1[...])
        x2h = x2.astype(BF16)
        q3[...] = mm_nt(x2h, e2[...])
        for k in range(4):
            v2[k] = x2h[16 * (k // 2) : 16 * (k // 2) + 16, 128 * (k % 2) : 128 * (k % 2) + 128]
        v1[...] = x1h

    pl.semaphore_wait(far_sem, 4)
    for copy in one[7:]:
        copy.wait_recv()
    x3h = (q3[...] + jnp.concatenate([line_sum(p3, 0), line_sum(p3, 1)], axis=1)).astype(BF16)
    for k in range(8):
        v3[k] = x3h[16 * (k // 4) : 16 * (k // 4) + 16, 128 * (k % 4) : 128 * (k % 4) + 128]

    two = []
    for j in ring:
        yy = y_peer(j)
        two.append(send(v3.at[yy], b3.at[j], p2_s.at[j], p2_r.at[j], at(x, yy, z, core)))
    for j in ring:
        yy = y_peer(j)
        two.append(send(v2.at[lax.rem(yy, 4)], b2.at[j], p2_s.at[8 + j], p2_r.at[8 + j], at(x, yy, z, core)))
    for j in range(1, 4):
        two.append(send(v1, b1.at[j], p2_s.at[16 + j], p2_r.at[16 + j], at(x, q_peer(j), z, core)))
    for copy in two[:14]:
        copy.start()

    g0 = mm_tn(f0, f0).astype(BF16)
    g1[...] = mm_tn(f1, f1).astype(BF16)
    g2[...] = mm_tn(f2, f2).astype(BF16)
    g3[...] = mm_tn(f3, f3).astype(BF16)
    yb[...] = jnp.zeros_like(yb)
    blank = jnp.zeros((32, 64), BF16)
    gap = jnp.zeros((32, 32), BF16)
    for p in range(2):
        rows = g0[32 * p : 32 * p + 32, :]
        yb[128 * p + 64 : 128 * p + 96, :] = jnp.concatenate([blank, rows[:, :32], gap, blank, rows[:, 32:], gap], axis=1)
    wt = w[...].astype(F32).T
    lane = lax.rem(lax.broadcasted_iota(jnp.int32, (128, 256), 1), 128)
    xb[...] = jnp.where(lane < 64, wt, -wt).astype(BF16)

    for copy in two[:7]:
        copy.wait_recv()
    sum3 = v3[y].astype(F32)
    for j in range(1, 8):
        sum3 = sum3 + b3[j].astype(F32)
    t3[...] = sum3.astype(BF16)
    three = []
    for j in ring:
        three.append(send(t3, h3.at[j], p3_s.at[j], p3_r.at[j], at(x, y, z_peer(j), core)))
    for copy in three:
        copy.start()
    for copy in two[7:14]:
        copy.wait_recv()
    sum2 = v2[q].astype(F32)
    for j in range(1, 8):
        sum2 = sum2 + b2[j].astype(F32)
    t2[...] = sum2.astype(BF16)
    three.append(send(t2, h2, p3_s.at[8], p3_r.at[8], at(x, y, z_near, core)))
    three[-1].start()
    for copy in two[14:]:
        copy.start()

    for i in range(3):
        lo, hi = 256 * i, 256 * (i + 1)
        direct[lo:hi, :] = mm_tn(a[lo:, lo:hi], ih[lo:, :])
    picked_rows = mm(onehot, cm[...]).astype(BF16)
    for i in range(3):
        lo, hi = 256 * i, 256 * (i + 1)
        nn[lo:hi, :] = mm(picked_rows[:, lo:], a[lo:, lo:hi]).T.astype(BF16)
    out_slot = lax.broadcasted_iota(jnp.int32, (480, WIDE), 0)
    nn[INNER:, :] = (slots((480, WIDE), 1) == out_slot).astype(BF16)
    for copy in fac_copies + one + two:
        copy.wait_send()

    for copy in three[:7]:
        copy.wait_recv()
    top = t3[...].astype(F32)
    for j in range(1, 8):
        top = top + h3[j].astype(F32)
    r3[y] = top.astype(BF16)
    four = []
    for j in ring:
        four.append(send(r3.at[y], r3.at[y], p4_s.at[j], p4_r.at[j], at(x, y_peer(j), z, core)))
    for copy in four:
        copy.start()
    three[7].wait_recv()
    r2[q] = (t2[...].astype(F32) + h2[...].astype(F32)).astype(BF16)
    for j in range(1, 4):
        four.append(send(r2.at[q], r2.at[q], p4_s.at[8 + j], p4_r.at[8 + j], at(x, q_peer(j), z, core)))
        four[-1].start()

    for copy in two[14:]:
        copy.wait_recv()
    low = v1[...].astype(F32)
    for j in range(1, 4):
        low = low + b1[j].astype(F32)
    own1 = mm(low.astype(BF16), g1[...])
    own0 = mm(tl[...], yb[...])
    for copy in three:
        copy.wait_send()
    for copy in four[7:]:
        copy.wait_recv()
    whole2 = jnp.concatenate(
        [jnp.concatenate([r2[2 * i], r2[2 * i + 1]], axis=1) for i in range(2)], axis=0
    )
    own2 = mm(whole2, g2[...])
    for copy in four[:7]:
        copy.wait_recv()
    whole3 = jnp.concatenate(
        [jnp.concatenate([r3[4 * i + k] for k in range(4)], axis=1) for i in range(2)], axis=0
    )
    d3 = mm(whole3, g3[...]).astype(BF16)
    for p in range(2):
        o3[p] = d3[:, 256 * p : 256 * p + 256]

    five = []
    for half, (source, target) in enumerate([(o3, d3a), (orr, dra)]):
        for j, (dx, dc) in enumerate(lines):
            xx, cc = x_peer(dx, dc)
            k = 7 * half + j
            five.append(send(source.at[cc], target.at[own], p5_s.at[k], p5_r.at[k], at(xx, y, z, cc)))
    for copy in five[:7]:
        copy.start()
    d3a[own] = o3[core]
    d2 = (own2 - mm(d3, e2[...])).astype(BF16)
    d1 = (own1 - mm(d2, e1[...])).astype(BF16)
    d0 = (own0 + mm(d1, xb[...])).astype(BF16)
    for p in range(2):
        orr[p] = jnp.concatenate([d2[:, 128 * p : 128 * p + 128], d0[:, 128 * p : 128 * p + 128]], axis=1)
    for copy in five[7:]:
        copy.start()
    dra[own] = orr[core]
    for copy in five[:7]:
        copy.wait_recv()
    down3 = d3a[...].reshape(SHOTS, 256)
    for i in range(3):
        lo, hi = 256 * i, 256 * (i + 1)
        direct[lo:hi, :] = direct[lo:hi, :] - mm_nt(nn[lo:hi, :256], down3)
    sep_ref[224:, :] = mm_nt(nn[INNER + 224 :, :256], down3).astype(BF16)
    for copy in five[7:]:
        copy.wait_recv()
    downr = dra[...].reshape(SHOTS, 256)
    for i in range(3):
        lo, hi = 256 * i, 256 * (i + 1)
        inner_ref[lo:hi, :] = (direct[lo:hi, :] - mm_nt(nn[lo:hi, 256:], downr)).astype(BF16)
    sep_ref[:224, :] = mm_nt(nn[INNER : INNER + 224, 256:], downr).astype(BF16)
    for copy in four + five:
        copy.wait_send()


def write_out(inner, sep, inner_h, sep_h, sem):
    copies = [
        pltpu.make_async_copy(inner, inner_h, sem.at[0]),
        pltpu.make_async_copy(sep, sep_h, sem.at[1]),
    ]
    for copy in copies:
        copy.start()
    for copy in copies:
        copy.wait()


def local(
    sources, inner_inv, coupling, boundary_map,
    sep_inv_0, sep_inv_1, sep_inv_2, sep_inv_3, sep_couple_0, sep_couple_1, sep_couple_2,
):
    held = [
        sources[0, 0], inner_inv[0, 0], coupling[0, 0], boundary_map[0],
        sep_inv_0[0], sep_inv_1[0], sep_inv_2[0], sep_inv_3[0],
        sep_couple_0[0], sep_couple_1[0], sep_couple_2[0],
    ]
    held = [pltpu.with_memory_space_constraint(v, pltpu.HBM) for v in held]
    hbm = pl.BlockSpec(memory_space=pltpu.HBM)
    vmem = pl.BlockSpec(memory_space=pltpu.VMEM)
    v = pltpu.VMEM
    dma = pltpu.SemaphoreType.DMA
    piece = v((X * C, OWN, 256), BF16)
    scratch = [
        v((INNER, SHOTS), BF16), v((INNER, INNER), BF16), v((BOUND, INNER), BF16), v((1, BOUND), jnp.int32),
        v((2, 32, 64), BF16), v((2, 64, 128), BF16), v((2, 128, 256), BF16), v((2, 256, 512), BF16),
        v((2, 64, 64), BF16), v((2, 128, 128), BF16), v((2, 256, 256), BF16),
        v((INNER, SHOTS), BF16), piece, piece, piece, piece,
        v((256, 128), BF16), v((128, 256), BF16), v((256, 256), BF16),
        v((256, 128), BF16), v((512, 256), BF16),
        v((128, 128), BF16), v((256, 256), BF16), v((512, 512), BF16),
        v((INNER + 480, WIDE), BF16), v((INNER, SHOTS), F32),
        v((OWN, 256), BF16), v((OWN, WIDE), F32),
        v((8, 16, 128), BF16), v((4, 16, 128), BF16), v((32, 128), BF16),
        v((8, 16, 128), BF16), v((8, 16, 128), BF16), v((4, 32, 128), BF16),
        v((16, 128), BF16), v((16, 128), BF16), v((8, 16, 128), BF16), v((16, 128), BF16),
        v((8, 16, 128), BF16), v((4, 16, 128), BF16),
        v((2, OWN, 256), BF16), v((2, OWN, 256), BF16), piece, piece,
        pltpu.SemaphoreType.REGULAR, dma((13,)), dma((7,)), dma((7,)), dma((14,)), dma((14,)), dma((20,)), dma((20,)),
        dma((9,)), dma((9,)), dma((12,)), dma((12,)), dma((14,)), dma((14,)),
    ]
    inner, sep = pl.pallas_call(
        kernel,
        out_shape=(
            jax.ShapeDtypeStruct((INNER, SHOTS), BF16),
            jax.ShapeDtypeStruct((480, SHOTS), BF16),
        ),
        in_specs=[hbm] * 11,
        out_specs=(vmem, vmem),
        scratch_shapes=scratch,
        compiler_params=pltpu.CompilerParams(
            collective_id=0, has_side_effects=True, vmem_limit_bytes=24 * 1024 * 1024
        ),
    )(*held)
    inner, sep = pl.pallas_call(
        write_out,
        out_shape=(
            jax.ShapeDtypeStruct((INNER, SHOTS), BF16),
            jax.ShapeDtypeStruct((480, SHOTS), BF16),
        ),
        in_specs=[vmem] * 2,
        out_specs=(pl.BlockSpec(memory_space=pltpu.HBM),) * 2,
        scratch_shapes=[dma((2,))],
        compiler_params=pltpu.CompilerParams(vmem_limit_bytes=8 * 1024 * 1024),
    )(inner, sep)
    return inner[None, None], sep[None, None]


def solution(mesh):
    leaf, factor = P("sub", "sep", None, None), P("sub", "sep", None)
    return jax.shard_map(
        local,
        mesh=mesh,
        in_specs=(leaf, leaf, leaf, factor) + (factor,) * 7,
        out_specs=(leaf, leaf),
        check_vma=False,
    )
```

```python
import functools

import jax
import jax.numpy as jnp
from jax import lax
from jax.experimental import pallas as pl
from jax.experimental.pallas import tpu as pltpu
from jax.sharding import PartitionSpec as P

MESH = pl.DeviceIdType.MESH
F32 = jnp.float32
BF16 = jnp.bfloat16
X, Y, Z, C = 4, 8, 8, 2
INNER, BOUND, SHOTS = 768, 512, 256
OWN = SHOTS // (X * C)
WIDE = 512


def mm(a, b):
    return lax.dot_general(a, b, (((1,), (0,)), ((), ())), preferred_element_type=F32)


def mm_nt(a, b):
    return lax.dot_general(a, b, (((1,), (1,)), ((), ())), preferred_element_type=F32)


def mm_tn(a, b):
    return lax.dot_general(a, b, (((0,), (0,)), ((), ())), preferred_element_type=F32)


def slots(shape, dim):
    at = lax.broadcasted_iota(jnp.int32, shape, dim)
    low = jnp.where(at < 448, at - 352, jnp.where(at < 480, at - 448, -1))
    return jnp.where(at < 256, at + 224, jnp.where(at < 384, at - 160, low))


def kernel(
    src_h, a_h, c_h, map_h, s0_h, s1_h, s2_h, s3_h, k0_h, k1_h, k2_h,
    inner_ref, sep_ref,
    src, a, cm, mp, s0, s1, s2, s3, k0, k1, k2,
    ih, lt3, ltr, p3, pr, w, xb, yb, e1, e2, g1, g2, g3, nn, direct,
    tl, q3, v3, v2, v1, b3, b2, b1, t3, t2, h3, h2, r3, r2, o3, orr, d3a, dra,
    far_sem, load_sem, fac_s, fac_r, p1_s, p1_r, p2_s, p2_r, p3_s, p3_r, p4_s, p4_r, p5_s, p5_r,
):
    sub = lax.axis_index("sub")
    core = lax.axis_index("sep")
    x = lax.rem(sub, X)
    y = lax.rem(sub // X, Y)
    z = sub // (X * Y)
    q = lax.rem(y, 4)
    quad = y - q
    own = x * C + core

    def at(xx, yy, zz, cc):
        return {"sub": zz * (X * Y) + yy * X + xx, "sep": cc}

    def x_peer(dx, dc):
        return lax.rem(x + dx, X), lax.rem(core + dc, C)

    def y_peer(j):
        return lax.rem(y + j, Y)

    def q_peer(j):
        return quad + lax.rem(q + j, 4)

    def z_peer(j):
        return lax.rem(z + j, Z)

    z_near = z + 1 - 2 * lax.rem(z, 2)
    lines = [(2, 0), (2, 1), (1, 0), (3, 0), (1, 1), (3, 1), (0, 1)]
    ring = [4, 3, 5, 2, 6, 1, 7]

    barrier = pltpu.get_barrier_semaphore()
    near = [2, 6, 1, 7]
    peers = [at(x_peer(dx, dc)[0], y, z, x_peer(dx, dc)[1]) for dx, dc in lines[:2]]
    peers += [at(x, y, z_peer(j), core) for j in near]
    peers += [at(x, y_peer(j), z, core) for j in near]
    peers += [at(x_peer(dx, dc)[0], y, z, x_peer(dx, dc)[1]) for dx, dc in lines[2:]]
    for peer in peers:
        pl.semaphore_signal(barrier, inc=1, device_id=peer, device_id_type=MESH)

    loads = [pltpu.make_async_copy(map_h, mp, load_sem.at[0])]
    loads.append(pltpu.make_async_copy(src_h, src, load_sem.at[1]))
    for i in range(3):
        lo, hi = 256 * i, 256 * (i + 1)
        loads.append(pltpu.make_async_copy(a_h.at[lo:hi, :hi], a.at[lo:hi, :hi], load_sem.at[2 + i]))
    loads.append(pltpu.make_async_copy(c_h, cm, load_sem.at[5]))
    facs = [(s0_h, s0), (s1_h, s1), (s2_h, s2), (s3_h, s3), (k0_h, k0), (k1_h, k1), (k2_h, k2)]
    for i, (h, v) in enumerate(facs):
        loads.append(pltpu.make_async_copy(h, v.at[core], load_sem.at[6 + i]))
    for copy in loads:
        copy.start()

    def send(source, target, s, r, peer):
        return pltpu.make_async_remote_copy(
            src_ref=source, dst_ref=target, send_sem=s, recv_sem=r, device_id=peer, device_id_type=MESH
        )

    loads[0].wait()
    onehot = (slots((WIDE, BOUND), 0) == mp[...]).astype(BF16)
    loads[1].wait()
    for i in range(3):
        lo, hi = 256 * i, 256 * (i + 1)
        loads[2 + i].wait()
        ih[lo:hi, :] = mm(a[lo:hi, :hi], src[:hi, :]).astype(BF16)
    loads[5].wait()
    bh = mm(cm[...], ih[...])
    bht = bh.T.astype(BF16)
    ltr[...] = mm_nt(bht, onehot[256:, :]).astype(BF16).reshape(X * C, OWN, 256)
    lt3[...] = mm_nt(bht, onehot[:256, :]).astype(BF16).reshape(X * C, OWN, 256)
    pl.semaphore_wait(barrier, len(peers))

    one = []
    for half, (source, target) in enumerate([(ltr, pr), (lt3, p3)]):
        for j, (dx, dc) in enumerate(lines):
            xx, cc = x_peer(dx, dc)
            k = 7 * half + j
            one.append(send(source.at[xx * C + cc], target.at[own], p1_s.at[k], p1_r.at[k], at(xx, y, z, cc)))
    for copy in one[:7]:
        copy.start()
    for copy in one[7:]:
        copy.start()
    for peer in [at(x, y, z_peer(2), core), at(x, y, z_peer(6), core), at(x, y_peer(2), z, core), at(x, y_peer(6), z, core)]:
        pl.semaphore_signal(far_sem, inc=1, device_id=peer, device_id_type=MESH)
    fac_copies = [
        send(h, v.at[core], fac_s.at[i], fac_r.at[i], at(x, y, z, 1 - core)) for i, (h, v) in enumerate(facs)
    ]
    for copy in fac_copies:
        copy.start()
    pr[own] = ltr[own]
    p3[own] = lt3[own]

    for copy in loads[6:]:
        copy.wait()
    for copy in fac_copies:
        copy.wait_recv()
    f0 = s0[...].reshape(64, 64)
    f1 = s1[...].reshape(128, 128)
    f2 = s2[...].reshape(256, 256)
    f3 = s3[...].reshape(512, 512)
    m0 = k0[...].reshape(128, 64)
    m1 = k1[...].reshape(256, 128)
    m2 = k2[...].reshape(512, 256)
    e0 = mm(m0, f0)
    e0t = e0.T.astype(BF16)
    e1[...] = mm(m1, f1).astype(BF16)
    e2[...] = mm(m2, f2).astype(BF16)
    w[...] = jnp.zeros_like(w)
    row = lax.broadcasted_iota(jnp.int32, (64, 128), 0)
    col = lax.broadcasted_iota(jnp.int32, (64, 128), 1)
    for p in range(2):
        w[128 * p : 128 * p + 64, :] = (col == row + 64 * p).astype(BF16)
        w[128 * p + 64 : 128 * p + 96, :] = e0t[32 * p : 32 * p + 32, :]

    def line_sum(buffer, p):
        total = buffer[p].astype(F32)
        for xx in range(1, X):
            total = total + buffer[xx * C + p].astype(F32)
        return total

    for copy in one[:7]:
        copy.wait_recv()

    @pl.when(sub < X * Y * Z)
    def _():
        rest = [line_sum(pr, p) for p in range(2)]
        tails = jnp.concatenate([rest[0][:, 128:], rest[1][:, 128:]], axis=1).astype(BF16)
        tl[...] = tails
        x1h = mm(tails, w[...]).astype(BF16)
        x2 = jnp.concatenate([rest[0][:, :128], rest[1][:, :128]], axis=1) + mm_nt(x1h, e1[...])
        x2h = x2.astype(BF16)
        q3[...] = mm_nt(x2h, e2[...])
        for k in range(4):
            v2[k] = x2h[16 * (k // 2) : 16 * (k // 2) + 16, 128 * (k % 2) : 128 * (k % 2) + 128]
        v1[...] = x1h

    pl.semaphore_wait(far_sem, 4)
    for copy in one[7:]:
        copy.wait_recv()
    x3h = (q3[...] + jnp.concatenate([line_sum(p3, 0), line_sum(p3, 1)], axis=1)).astype(BF16)
    for k in range(8):
        v3[k] = x3h[16 * (k // 4) : 16 * (k // 4) + 16, 128 * (k % 4) : 128 * (k % 4) + 128]

    two = []
    for j in ring:
        yy = y_peer(j)
        two.append(send(v3.at[yy], b3.at[j], p2_s.at[j], p2_r.at[j], at(x, yy, z, core)))
    for j in ring:
        yy = y_peer(j)
        two.append(send(v2.at[lax.rem(yy, 4)], b2.at[j], p2_s.at[8 + j], p2_r.at[8 + j], at(x, yy, z, core)))
    for j in range(1, 4):
        two.append(send(v1, b1.at[j], p2_s.at[16 + j], p2_r.at[16 + j], at(x, q_peer(j), z, core)))
    for copy in two[:14]:
        copy.start()

    @pl.when(sub < X * Y * Z)
    def _():
        g0 = mm_tn(f0, f0).astype(BF16)
        g1[...] = mm_tn(f1, f1).astype(BF16)
        g2[...] = mm_tn(f2, f2).astype(BF16)
        g3[...] = mm_tn(f3, f3).astype(BF16)
        yb[...] = jnp.zeros_like(yb)
        blank = jnp.zeros((32, 64), BF16)
        gap = jnp.zeros((32, 32), BF16)
        for p in range(2):
            rows = g0[32 * p : 32 * p + 32, :]
            yb[128 * p + 64 : 128 * p + 96, :] = jnp.concatenate([blank, rows[:, :32], gap, blank, rows[:, 32:], gap], axis=1)
        wt = w[...].astype(F32).T
        lane = lax.rem(lax.broadcasted_iota(jnp.int32, (128, 256), 1), 128)
        xb[...] = jnp.where(lane < 64, wt, -wt).astype(BF16)

    for copy in two[:7]:
        copy.wait_recv()
    sum3 = v3[y].astype(F32)
    for j in range(1, 8):
        sum3 = sum3 + b3[j].astype(F32)
    t3[...] = sum3.astype(BF16)
    three = []
    for j in ring:
        three.append(send(t3, h3.at[j], p3_s.at[j], p3_r.at[j], at(x, y, z_peer(j), core)))
    for copy in three:
        copy.start()
    for copy in two[7:14]:
        copy.wait_recv()
    sum2 = v2[q].astype(F32)
    for j in range(1, 8):
        sum2 = sum2 + b2[j].astype(F32)
    t2[...] = sum2.astype(BF16)
    three.append(send(t2, h2, p3_s.at[8], p3_r.at[8], at(x, y, z_near, core)))
    three[-1].start()
    for copy in two[14:]:
        copy.start()

    for i in range(3):
        lo, hi = 256 * i, 256 * (i + 1)
        direct[lo:hi, :] = mm_tn(a[lo:, lo:hi], ih[lo:, :])
    picked_rows = mm(onehot, cm[...]).astype(BF16)
    for i in range(3):
        lo, hi = 256 * i, 256 * (i + 1)
        nn[lo:hi, :] = mm(picked_rows[:, lo:], a[lo:, lo:hi]).T.astype(BF16)
    out_slot = lax.broadcasted_iota(jnp.int32, (480, WIDE), 0)
    nn[INNER:, :] = (slots((480, WIDE), 1) == out_slot).astype(BF16)
    for copy in fac_copies + one + two:
        copy.wait_send()

    for copy in three[:7]:
        copy.wait_recv()
    top = t3[...].astype(F32)
    for j in range(1, 8):
        top = top + h3[j].astype(F32)
    r3[y] = top.astype(BF16)
    four = []
    for j in ring:
        four.append(send(r3.at[y], r3.at[y], p4_s.at[j], p4_r.at[j], at(x, y_peer(j), z, core)))
    for copy in four:
        copy.start()
    three[7].wait_recv()
    r2[q] = (t2[...].astype(F32) + h2[...].astype(F32)).astype(BF16)
    for j in range(1, 4):
        four.append(send(r2.at[q], r2.at[q], p4_s.at[8 + j], p4_r.at[8 + j], at(x, q_peer(j), z, core)))
        four[-1].start()

    for copy in two[14:]:
        copy.wait_recv()
    low = v1[...].astype(F32)
    for j in range(1, 4):
        low = low + b1[j].astype(F32)
    own1 = mm(low.astype(BF16), g1[...])
    own0 = mm(tl[...], yb[...])
    for copy in three:
        copy.wait_send()
    for copy in four[7:]:
        copy.wait_recv()
    whole2 = jnp.concatenate(
        [jnp.concatenate([r2[2 * i], r2[2 * i + 1]], axis=1) for i in range(2)], axis=0
    )
    own2 = mm(whole2, g2[...])
    for copy in four[:7]:
        copy.wait_recv()
    whole3 = jnp.concatenate(
        [jnp.concatenate([r3[4 * i + k] for k in range(4)], axis=1) for i in range(2)], axis=0
    )
    d3 = mm(whole3, g3[...]).astype(BF16)
    for p in range(2):
        o3[p] = d3[:, 256 * p : 256 * p + 256]

    five = []
    for half, (source, target) in enumerate([(o3, d3a), (orr, dra)]):
        for j, (dx, dc) in enumerate(lines):
            xx, cc = x_peer(dx, dc)
            k = 7 * half + j
            five.append(send(source.at[cc], target.at[own], p5_s.at[k], p5_r.at[k], at(xx, y, z, cc)))
    for copy in five[:7]:
        copy.start()
    d3a[own] = o3[core]
    d2 = (own2 - mm(d3, e2[...])).astype(BF16)
    d1 = (own1 - mm(d2, e1[...])).astype(BF16)
    d0 = (own0 + mm(d1, xb[...])).astype(BF16)
    for p in range(2):
        orr[p] = jnp.concatenate([d2[:, 128 * p : 128 * p + 128], d0[:, 128 * p : 128 * p + 128]], axis=1)
    for copy in five[7:]:
        copy.start()
    dra[own] = orr[core]
    for copy in five[:7]:
        copy.wait_recv()
    down3 = d3a[...].reshape(SHOTS, 256)
    for i in range(3):
        lo, hi = 256 * i, 256 * (i + 1)
        direct[lo:hi, :] = direct[lo:hi, :] - mm_nt(nn[lo:hi, :256], down3)
    sep_ref[224:, :] = mm_nt(nn[INNER + 224 :, :256], down3).astype(BF16)
    for copy in five[7:]:
        copy.wait_recv()
    downr = dra[...].reshape(SHOTS, 256)
    for i in range(3):
        lo, hi = 256 * i, 256 * (i + 1)
        inner_ref[lo:hi, :] = (direct[lo:hi, :] - mm_nt(nn[lo:hi, 256:], downr)).astype(BF16)
    sep_ref[:224, :] = mm_nt(nn[INNER : INNER + 224, 256:], downr).astype(BF16)
    for copy in four + five:
        copy.wait_send()


def write_out(inner, sep, inner_h, sep_h, sem):
    copies = [
        pltpu.make_async_copy(inner, inner_h, sem.at[0]),
        pltpu.make_async_copy(sep, sep_h, sem.at[1]),
    ]
    for copy in copies:
        copy.start()
    for copy in copies:
        copy.wait()


def local(
    sources, inner_inv, coupling, boundary_map,
    sep_inv_0, sep_inv_1, sep_inv_2, sep_inv_3, sep_couple_0, sep_couple_1, sep_couple_2,
):
    held = [
        sources[0, 0], inner_inv[0, 0], coupling[0, 0], boundary_map[0],
        sep_inv_0[0], sep_inv_1[0], sep_inv_2[0], sep_inv_3[0],
        sep_couple_0[0], sep_couple_1[0], sep_couple_2[0],
    ]
    held = [pltpu.with_memory_space_constraint(v, pltpu.HBM) for v in held]
    hbm = pl.BlockSpec(memory_space=pltpu.HBM)
    vmem = pl.BlockSpec(memory_space=pltpu.VMEM)
    v = pltpu.VMEM
    dma = pltpu.SemaphoreType.DMA
    piece = v((X * C, OWN, 256), BF16)
    scratch = [
        v((INNER, SHOTS), BF16), v((INNER, INNER), BF16), v((BOUND, INNER), BF16), v((1, BOUND), jnp.int32),
        v((2, 32, 64), BF16), v((2, 64, 128), BF16), v((2, 128, 256), BF16), v((2, 256, 512), BF16),
        v((2, 64, 64), BF16), v((2, 128, 128), BF16), v((2, 256, 256), BF16),
        v((INNER, SHOTS), BF16), piece, piece, piece, piece,
        v((256, 128), BF16), v((128, 256), BF16), v((256, 256), BF16),
        v((256, 128), BF16), v((512, 256), BF16),
        v((128, 128), BF16), v((256, 256), BF16), v((512, 512), BF16),
        v((INNER + 480, WIDE), BF16), v((INNER, SHOTS), F32),
        v((OWN, 256), BF16), v((OWN, WIDE), F32),
        v((8, 16, 128), BF16), v((4, 16, 128), BF16), v((32, 128), BF16),
        v((8, 16, 128), BF16), v((8, 16, 128), BF16), v((4, 32, 128), BF16),
        v((16, 128), BF16), v((16, 128), BF16), v((8, 16, 128), BF16), v((16, 128), BF16),
        v((8, 16, 128), BF16), v((4, 16, 128), BF16),
        v((2, OWN, 256), BF16), v((2, OWN, 256), BF16), piece, piece,
        pltpu.SemaphoreType.REGULAR, dma((13,)), dma((7,)), dma((7,)), dma((14,)), dma((14,)), dma((20,)), dma((20,)),
        dma((9,)), dma((9,)), dma((12,)), dma((12,)), dma((14,)), dma((14,)),
    ]
    inner, sep = pl.pallas_call(
        kernel,
        out_shape=(
            jax.ShapeDtypeStruct((INNER, SHOTS), BF16),
            jax.ShapeDtypeStruct((480, SHOTS), BF16),
        ),
        in_specs=[hbm] * 11,
        out_specs=(vmem, vmem),
        scratch_shapes=scratch,
        compiler_params=pltpu.CompilerParams(
            collective_id=0, has_side_effects=True, vmem_limit_bytes=24 * 1024 * 1024
        ),
    )(*held)
    inner, sep = pl.pallas_call(
        write_out,
        out_shape=(
            jax.ShapeDtypeStruct((INNER, SHOTS), BF16),
            jax.ShapeDtypeStruct((480, SHOTS), BF16),
        ),
        in_specs=[vmem] * 2,
        out_specs=(pl.BlockSpec(memory_space=pltpu.HBM),) * 2,
        scratch_shapes=[dma((2,))],
        compiler_params=pltpu.CompilerParams(vmem_limit_bytes=8 * 1024 * 1024),
    )(inner, sep)
    return inner[None, None], sep[None, None]


def solution(mesh):
    leaf, factor = P("sub", "sep", None, None), P("sub", "sep", None)
    return jax.shard_map(
        local,
        mesh=mesh,
        in_specs=(leaf, leaf, leaf, factor) + (factor,) * 7,
        out_specs=(leaf, leaf),
        check_vma=False,
    )
```
